32 devices in a mesh: grp: 16 (over z, y, core), half: 2 (over x).
Axes of the slice: x: 2, y: 2, z: 4, core: 2. Of those that a mesh axis runs over, the one named last changes fastest.
Arguments:
- field: bfloat16 [16, 2, 1024, 512], P('grp', 'half'), may hold values from -6 to 6
- source_one: bfloat16 [16, 2, 4, 256, 256], P('grp', 'half'), may hold values from -0.375 to 0.375
- sections_one: bfloat16 [16, 2, 3, 4, 256, 512], P('grp', 'half'), may hold values from -0.25 to 0.25
- target_one: bfloat16 [16, 2, 4, 256, 256], P('grp', 'half'), may hold values from -0.375 to 0.375
- source_two: bfloat16 [16, 2, 4, 256, 256], P('grp', 'half'), may hold values from -0.375 to 0.375
- sections_two: bfloat16 [16, 2, 3, 4, 256, 512], P('grp', 'half'), may hold values from -0.25 to 0.25
- target_two: bfloat16 [16, 2, 4, 256, 256], P('grp', 'half'), may hold values from -0.375 to 0.375
- pairing: int32 [2, 3, 16, 2, 4], P(None, None, 'grp', 'half'), may hold values from 0 to 3, each once within a row
Outputs:
- scattered: bfloat16 [16, 2, 1024, 512], P('grp', 'half')
The draws below stay inside these ranges and needn't reach their ends.
Inputs may be any that keep to these rules, and one draw needn't show every extreme that they name: For every level l, section s, group index g and half h, pairing[l, s, g, h] is a permutation of the 4 nodes.
All inputs are finite; a program needn't handle non-finite values.
Results may differ from the reference program's by a relative error of at most 0.007.
Values may be sent and summed in bfloat16 or wider, within the bound.
No kernel may reach another device: no remote copies, remote signals or barrier semaphores. Data moves between devices by JAX's collectives and lax.ppermute only.
A program may use at most 64 MiB of HBM per device.

```python
import jax
import jax.numpy as jnp
import numpy as np

LEAF = 256
COLS = 512
NODES = 4
SECTIONS = 3
N_GRP = 16


def level_of(stream_key, dims, cuts, least, top_value):
    loudness = 1.0
    for axis_at, blocks in cuts:
        steps = jax.random.uniform(jax.random.fold_in(jax.random.fold_in(stream_key, 6), axis_at), (blocks,), jnp.float32, least / len(cuts), top_value / len(cuts))
        loudness = loudness * jnp.repeat(jnp.exp(steps), dims[axis_at] // blocks).reshape((-1,) + (1,) * (len(dims) - 1 - axis_at))
    return loudness


def normal_values(stream_key, dims, width, bound, pieces=(), kind=jnp.bfloat16):
    loudness = level_of(stream_key, dims, pieces, -0.22, 0.18) if pieces else 1.0
    array = jax.random.normal(stream_key, dims, jnp.float32) * width * loudness
    return jnp.minimum(jnp.maximum(array, -bound), bound).astype(kind)


def setup_inputs(seed: int = 0) -> dict:
    seeds = jax.random.split(jax.random.key(seed), 9)
    return {
        "field": normal_values(seeds[0], (N_GRP, 2, NODES * LEAF, COLS), 1.0, 6.0, ((0, 16), (1, 2))),
        "source_one": normal_values(seeds[1], (N_GRP, 2, NODES, LEAF, LEAF), LEAF ** -0.5, 0.375, ((0, 16), (1, 2))),
        "sections_one": normal_values(seeds[2], (N_GRP, 2, SECTIONS, NODES, LEAF, 2 * LEAF), (2 * LEAF) ** -0.5, 0.25, ((0, 16), (1, 2))),
        "target_one": normal_values(seeds[3], (N_GRP, 2, NODES, LEAF, LEAF), LEAF ** -0.5, 0.375, ((0, 16), (1, 2))),
        "source_two": normal_values(seeds[4], (N_GRP, 2, NODES, LEAF, LEAF), LEAF ** -0.5, 0.375, ((0, 16), (1, 2))),
        "sections_two": normal_values(seeds[5], (N_GRP, 2, SECTIONS, NODES, LEAF, 2 * LEAF), (2 * LEAF) ** -0.5, 0.25, ((0, 16), (1, 2))),
        "target_two": normal_values(seeds[6], (N_GRP, 2, NODES, LEAF, LEAF), LEAF ** -0.5, 0.375, ((0, 16), (1, 2))),
        "pairing": jax.vmap(lambda own: jax.random.permutation(own, NODES))(jax.random.split(seeds[7], 2 * SECTIONS * N_GRP * 2)).reshape((2, SECTIONS, N_GRP, 2, NODES)).astype(jnp.int32),
    }


def leaf_product(basis, blocks):
    return jnp.einsum('ghnij,ghnjc->ghnic', basis.astype(jnp.float32), blocks.astype(jnp.float32))


def run_sections(coeffs, weights, tables, first_bit):
    for section in range(SECTIONS):
        partner_rows = np.arange(N_GRP) ^ (1 << (first_bit - section))
        partner = coeffs[partner_rows]
        index = jnp.broadcast_to(tables[section].astype(jnp.int32)[:, :, :, None, None], partner.shape)
        partner = jnp.take_along_axis(partner, index, axis=2)
        stacked = jnp.concatenate([coeffs, partner], axis=3)
        coeffs = leaf_product(weights[:, :, section], stacked).astype(jnp.bfloat16)
    return coeffs


def reference(field, source_one, sections_one, target_one, source_two, sections_two, target_two, pairing):
    top_bit = N_GRP.bit_length() - 1
    shaped = field.reshape(N_GRP, 2, NODES, LEAF, COLS)
    first = run_sections(leaf_product(source_one, shaped).astype(jnp.bfloat16), sections_one, pairing[0], top_bit - 1)
    second = run_sections(leaf_product(source_two, shaped).astype(jnp.bfloat16), sections_two, pairing[1], top_bit - 2)
    far_rows = np.arange(N_GRP) ^ (N_GRP // 2)
    total = leaf_product(target_one, first[:, ::-1]) + leaf_product(target_two, second[far_rows])
    return total.astype(jnp.bfloat16).reshape(N_GRP, 2, NODES * LEAF, COLS)
```

```python
import functools

import jax
import jax.numpy as jnp
from jax import lax
from jax.experimental import pallas as pl
from jax.experimental.pallas import tpu as pltpu
from jax.sharding import PartitionSpec as P

CHUNKS = 4


def swapped(value, axis, bit):
    return lax.ppermute(value, axis, [(i, i ^ 1 << bit) for i in range(lax.axis_size(axis))])


def dot(a, b):
    return jnp.dot(a, b, preferred_element_type=jnp.float32)


def cost(flops, *arrays):
    size = sum(a.size * a.dtype.itemsize for a in arrays)
    return pl.CostEstimate(flops=flops, bytes_accessed=size, transcendentals=0)


def source_kernel(x_ref, one_ref, two_ref, a_ref, b_ref):
    x = x_ref[0, 0]
    a_ref[0] = dot(one_ref[0, 0, 0], x).astype(a_ref.dtype)
    b_ref[0] = dot(two_ref[0, 0, 0], x).astype(b_ref.dtype)


def sources(field, one, two, chunk, width):
    nodes, leaf = one.shape[2:4]
    out = jax.ShapeDtypeStruct((nodes, leaf, width), jnp.bfloat16)
    basis = pl.BlockSpec((1, 1, 1, leaf, leaf), lambda n: (0, 0, n, 0, 0))
    piece = pl.BlockSpec((1, leaf, width), lambda n: (n, 0, 0))
    return pl.pallas_call(
        source_kernel,
        grid=(nodes,),
        out_shape=(out, out),
        in_specs=[pl.BlockSpec((1, 1, leaf, width), lambda n: (0, 0, n, chunk)), basis, basis],
        out_specs=(piece, piece),
        cost_estimate=cost(4 * nodes * leaf * leaf * width, out, out, out, one, two),
    )(field, one, two)


def section_kernel(table_ref, own_ref, partner_ref, w_ref, o_ref):
    leaf = own_ref.shape[1]
    w = w_ref[0, 0, 0, 0]
    total = dot(w[:, :leaf], own_ref[0]) + dot(w[:, leaf:], partner_ref[0])
    o_ref[0] = total.astype(o_ref.dtype)


def advance(own, partner, weights, table, level, section):
    nodes, leaf, width = own.shape
    sections = weights.shape[2]
    at = (level * sections + section) * nodes
    piece = pl.BlockSpec((1, leaf, width), lambda n, t: (n, 0, 0))
    return pl.pallas_call(
        section_kernel,
        grid_spec=pltpu.PrefetchScalarGridSpec(
            num_scalar_prefetch=1,
            grid=(nodes,),
            in_specs=[
                piece,
                pl.BlockSpec((1, leaf, width), lambda n, t: (t[at + n], 0, 0)),
                pl.BlockSpec(
                    (1, 1, 1, 1, leaf, 2 * leaf), lambda n, t: (0, 0, section, n, 0, 0)
                ),
            ],
            out_specs=piece,
        ),
        out_shape=jax.ShapeDtypeStruct(own.shape, own.dtype),
        cost_estimate=cost(4 * nodes * leaf * leaf * width, own, own, own, own, own, own, own),
    )(table, own, partner, weights)


def target_kernel(a_ref, b_ref, one_ref, two_ref, *refs):
    o_ref = refs[-1]
    total = dot(one_ref[0, 0, 0], a_ref[0]) + dot(two_ref[0, 0, 0], b_ref[0])
    o_ref[0, 0] = total.astype(o_ref.dtype)


def targets(sibling, distant, one, two, chunk, shape, held):
    nodes, leaf, width = sibling.shape
    basis = pl.BlockSpec((1, 1, 1, leaf, leaf), lambda n: (0, 0, n, 0, 0))
    piece = pl.BlockSpec((1, leaf, width), lambda n: (n, 0, 0))
    args = (sibling, distant, one, two)
    specs = [piece, piece, basis, basis]
    alias = {}
    if held is not None:
        args += (held,)
        specs.append(pl.BlockSpec(memory_space=pl.ANY))
        alias = {4: 0}
    return pl.pallas_call(
        target_kernel,
        grid=(nodes,),
        out_shape=jax.ShapeDtypeStruct(shape, jnp.bfloat16),
        in_specs=specs,
        out_specs=pl.BlockSpec((1, 1, leaf, width), lambda n: (0, 0, n, chunk)),
        input_output_aliases=alias,
        cost_estimate=cost(4 * nodes * leaf * leaf * width, sibling, distant, sibling, one, two),
    )(*args)


def on_device(
    field, source_one, sections_one, target_one, source_two, sections_two, target_two, pairing
):
    width = field.shape[3] // CHUNKS
    top_bit = lax.axis_size("grp").bit_length() - 1
    table = pairing.reshape(-1)
    first, second = [], []
    for k in range(CHUNKS):
        a, b = sources(field, source_one, source_two, k, width)
        first.append(a)
        second.append(b)
    for s in range(sections_one.shape[2]):
        for k in range(CHUNKS):
            other = swapped(first[k], "grp", top_bit - 1 - s)
            first[k] = advance(first[k], other, sections_one, table, 0, s)
            other = swapped(second[k], "grp", top_bit - 2 - s)
            second[k] = advance(second[k], other, sections_two, table, 1, s)
    out = None
    for k in range(CHUNKS):
        sibling = swapped(first[k], "half", 0)
        distant = swapped(second[k], "grp", top_bit - 1)
        out = targets(sibling, distant, target_one, target_two, k, field.shape, out)
    return out


def solution(mesh):
    placed = (
        P("grp", "half", None, None),
        P("grp", "half", None, None, None),
        P("grp", "half", None, None, None, None),
        P("grp", "half", None, None, None),
        P("grp", "half", None, None, None),
        P("grp", "half", None, None, None, None),
        P("grp", "half", None, None, None),
        P(None, None, "grp", "half", None),
    )
    return jax.shard_map(
        on_device,
        mesh=mesh,
        in_specs=placed,
        out_specs=P("grp", "half", None, None),
        check_vma=False,
    )
```

```python
import jax
import jax.numpy as jnp
from jax import lax
from jax.experimental import pallas as pl
from jax.experimental.pallas import tpu as pltpu
from jax.sharding import PartitionSpec as P

CHUNKS = 4
VMEM = pl.BlockSpec(memory_space=pltpu.VMEM)
SMEM = pl.BlockSpec(memory_space=pltpu.SMEM)


def swapped(value, axis, bit):
    return lax.ppermute(value, axis, [(i, i ^ 1 << bit) for i in range(lax.axis_size(axis))])


def small(mib=12):
    return pltpu.CompilerParams(vmem_limit_bytes=mib * 1024 * 1024)


def dot(a, b):
    return jnp.dot(a, b, preferred_element_type=jnp.float32)


def cost(products, shape):
    nodes, leaf, width = shape
    return pl.CostEstimate(
        flops=2 * products * nodes * leaf * leaf * width,
        bytes_accessed=2 * nodes * leaf * (2 * width + products * leaf),
        transcendentals=0,
    )


def source(field, basis, chunk, width):
    nodes, leaf = basis.shape[2:4]

    def kernel(x_ref, s_ref, o_ref):
        for n in range(nodes):
            x = x_ref[0, 0, pl.ds(n * leaf, leaf), pl.ds(chunk * width, width)]
            o_ref[n] = dot(s_ref[0, 0, n], x).astype(o_ref.dtype)

    out = jax.ShapeDtypeStruct((nodes, leaf, width), jnp.bfloat16)
    return pl.pallas_call(
        kernel, out_shape=out, in_specs=[VMEM, VMEM], out_specs=VMEM,
        cost_estimate=cost(1, out.shape), compiler_params=small(),
    )(field, basis)


def advance(own, partner, weights, table, level, section):
    nodes, leaf, width = own.shape

    def kernel(table_ref, own_ref, partner_ref, w_ref, o_ref):
        for n in range(nodes):
            w = w_ref[0, 0, section, n]
            other = partner_ref[table_ref[level, section, n]]
            total = dot(w[:, :leaf], own_ref[n]) + dot(w[:, leaf:], other)
            o_ref[n] = total.astype(o_ref.dtype)

    return pl.pallas_call(
        kernel, out_shape=jax.ShapeDtypeStruct(own.shape, own.dtype),
        in_specs=[SMEM, VMEM, VMEM, VMEM], out_specs=VMEM,
        cost_estimate=cost(2, own.shape), compiler_params=small(),
    )(table, own, partner, weights)


def target(sibling, distant, one, two, chunk, shape, held):
    nodes, leaf, width = sibling.shape

    def kernel(a_ref, b_ref, one_ref, two_ref, *refs):
        o_ref = refs[-1]
        for n in range(nodes):
            total = dot(one_ref[0, 0, n], a_ref[n]) + dot(two_ref[0, 0, n], b_ref[n])
            o_ref[0, 0, pl.ds(n * leaf, leaf), :] = total.astype(o_ref.dtype)

    args = (sibling, distant, one, two)
    specs = [VMEM] * 4
    alias = {}
    if held is not None:
        args += (held,)
        specs.append(pl.BlockSpec(memory_space=pl.ANY))
        alias = {4: 0}
    return pl.pallas_call(
        kernel, grid=(1,), out_shape=jax.ShapeDtypeStruct(shape, jnp.bfloat16),
        in_specs=specs,
        out_specs=pl.BlockSpec((1, 1, nodes * leaf, width), lambda i: (0, 0, 0, chunk)),
        input_output_aliases=alias,
        cost_estimate=cost(2, sibling.shape), compiler_params=small(),
    )(*args)


def on_device(
    field, source_one, sections_one, target_one, source_two, sections_two, target_two, pairing
):
    width = field.shape[3] // CHUNKS
    top_bit = lax.axis_size("grp").bit_length() - 1
    table = pairing[:, :, 0, 0]
    first, second = [], []
    for k in range(CHUNKS):
        first.append(source(field, source_one, k, width))
        second.append(source(field, source_two, k, width))
    for s in range(sections_one.shape[2]):
        for k in range(CHUNKS):
            other = swapped(first[k], "grp", top_bit - 1 - s)
            first[k] = advance(first[k], other, sections_one, table, 0, s)
            other = swapped(second[k], "grp", top_bit - 2 - s)
            second[k] = advance(second[k], other, sections_two, table, 1, s)
    out = None
    for k in range(CHUNKS):
        sibling = swapped(first[k], "half", 0)
        distant = swapped(second[k], "grp", top_bit - 1)
        out = target(sibling, distant, target_one, target_two, k, field.shape, out)
    return out


def solution(mesh):
    placed = (
        P("grp", "half", None, None),
        P("grp", "half", None, None, None),
        P("grp", "half", None, None, None, None),
        P("grp", "half", None, None, None),
        P("grp", "half", None, None, None),
        P("grp", "half", None, None, None, None),
        P("grp", "half", None, None, None),
        P(None, None, "grp", "half", None),
    )
    return jax.shard_map(
        on_device,
        mesh=mesh,
        in_specs=placed,
        out_specs=P("grp", "half", None, None),
        check_vma=False,
    )
```

```python
import jax
import jax.numpy as jnp
from jax import lax
from jax.experimental import pallas as pl
from jax.experimental.pallas import tpu as pltpu
from jax.sharding import PartitionSpec as P


CHUNKS = 4
VMEM = pl.BlockSpec(memory_space=pltpu.VMEM)
SMEM = pl.BlockSpec(memory_space=pltpu.SMEM)
ORDER = (
    (2, 0, 2), (2, 0, 1), (1, 0, 3), (2, 0, 3), (1, 0, 1), (1, 1, 3),
    (1, 0, 2), (2, 0, 0), (1, 0, 0), (2, 1, 2), (1, 1, 1), (2, 1, 1),
    (2, 2, 2), (2, 1, 3), (1, 2, 3), (2, 3, 2), (2, 2, 1), (2, 2, 3),
    (2, 1, 0), (1, 1, 2), (1, 3, 3), (1, 1, 0), (2, 3, 3), (2, 2, 0),
    (2, 3, 1), (1, 2, 1), (2, 3, 0), (1, 2, 2), (1, 3, 1), (1, 2, 0),
    (1, 3, 2), (1, 3, 0), (0, 0, 3), (0, 0, 2), (0, 0, 1), (0, 0, 0),
)


def swapped(value, axis, bit):
    return lax.ppermute(value, axis, [(i, i ^ 1 << bit) for i in range(lax.axis_size(axis))])


def dot(a, b):
    return jnp.dot(a, b, preferred_element_type=jnp.float32)


def small(mib=12):
    return pltpu.CompilerParams(vmem_limit_bytes=mib * 1024 * 1024)


def cost(products, shape):
    nodes, leaf, width = shape
    return pl.CostEstimate(
        flops=2 * products * nodes * leaf * leaf * width,
        bytes_accessed=2 * nodes * leaf * (2 * width + products * leaf),
        transcendentals=0,
    )


def source(field, basis, chunk, width):
    nodes, leaf = basis.shape[2:4]

    def kernel(x_ref, s_ref, o_ref):
        for n in range(nodes):
            x = x_ref[0, 0, pl.ds(n * leaf, leaf), pl.ds(chunk * width, width)]
            o_ref[n] = dot(s_ref[0, 0, n], x).astype(o_ref.dtype)

    out = jax.ShapeDtypeStruct((nodes, leaf, width), jnp.bfloat16)
    return pl.pallas_call(
        kernel, out_shape=out, in_specs=[VMEM, VMEM], out_specs=VMEM,
        cost_estimate=cost(1, out.shape), compiler_params=small(),
    )(field, basis)


def advance(own, partner, weights, table, level, section):
    nodes, leaf, _ = own.shape

    def kernel(table_ref, own_ref, partner_ref, w_ref, o_ref):
        for n in range(nodes):
            w = w_ref[0, 0, section, n]
            other = partner_ref[table_ref[level, section, n]]
            total = dot(w[:, :leaf], own_ref[n]) + dot(w[:, leaf:], other)
            o_ref[n] = total.astype(o_ref.dtype)

    return pl.pallas_call(
        kernel, out_shape=jax.ShapeDtypeStruct(own.shape, own.dtype),
        in_specs=[SMEM, VMEM, VMEM, VMEM], out_specs=VMEM,
        cost_estimate=cost(2, own.shape), compiler_params=small(),
    )(table, own, partner, weights)


def target(sibling, distant, one, two, chunk, shape, held):
    nodes, leaf, width = sibling.shape

    def kernel(a_ref, b_ref, one_ref, two_ref, *refs):
        o_ref = refs[-1]
        for n in range(nodes):
            total = dot(one_ref[0, 0, n], a_ref[n]) + dot(two_ref[0, 0, n], b_ref[n])
            o_ref[0, 0, pl.ds(n * leaf, leaf), :] = total.astype(o_ref.dtype)

    args = (sibling, distant, one, two)
    specs = [VMEM] * 4
    alias = {}
    if held is not None:
        args += (held,)
        specs.append(pl.BlockSpec(memory_space=pl.ANY))
        alias = {4: 0}
    return pl.pallas_call(
        kernel, grid=(1,), out_shape=jax.ShapeDtypeStruct(shape, jnp.bfloat16),
        in_specs=specs,
        out_specs=pl.BlockSpec((1, 1, nodes * leaf, width), lambda i: (0, 0, 0, chunk)),
        input_output_aliases=alias,
        cost_estimate=cost(2, sibling.shape), compiler_params=small(),
    )(*args)


def on_device(
    field, source_one, sections_one, target_one, source_two, sections_two, target_two, pairing
):
    width = field.shape[3] // CHUNKS
    top = lax.axis_size("grp").bit_length() - 1
    table = pairing[:, :, 0, 0]
    sources = {1: source_one, 2: source_two}
    sections = {1: sections_one, 2: sections_two}
    last = sections_one.shape[2]
    value, moved = {}, {}
    out = None
    for step in ORDER:
        level, stage, k = step
        if level == 0:
            out = target(moved[1, k], moved[2, k], target_one, target_two, k, field.shape, out)
        elif stage == 0:
            value[level, k] = source(field, sources[level], k, width)
        else:
            value[level, k] = advance(
                value[level, k], moved[level, k], sections[level], table,
                level - 1, stage - 1,
            )
        if level:
            if stage < last:
                axis, bit = "grp", top - level - stage
            else:
                axis, bit = ("half", 0) if level == 1 else ("grp", top - 1)
            moved[level, k] = swapped(value[level, k], axis, bit)
    return out


def solution(mesh):
    placed = (
        P("grp", "half", None, None),
        P("grp", "half", None, None, None),
        P("grp", "half", None, None, None, None),
        P("grp", "half", None, None, None),
        P("grp", "half", None, None, None),
        P("grp", "half", None, None, None, None),
        P("grp", "half", None, None, None),
        P(None, None, "grp", "half", None),
    )
    return jax.shard_map(
        on_device,
        mesh=mesh,
        in_specs=placed,
        out_specs=P("grp", "half", None, None),
        check_vma=False,
    )
```

```python
import jax
import jax.numpy as jnp
from jax import lax
from jax.experimental import pallas as pl
from jax.experimental.pallas import tpu as pltpu
from jax.sharding import PartitionSpec as P


CHUNKS = 4
VMEM = pl.BlockSpec(memory_space=pltpu.VMEM)
SMEM = pl.BlockSpec(memory_space=pltpu.SMEM)
HBM = pl.BlockSpec(memory_space=pltpu.HBM)
ORDER = (
    (2, 0, 2), (1, 0, 3), (3, 0, 0), (2, 0, 1), (2, 1, 2), (1, 0, 0),
    (1, 1, 3), (2, 0, 3), (1, 0, 1), (2, 1, 1), (2, 0, 0), (3, 2, 0),
    (1, 0, 2), (1, 1, 0), (2, 1, 3), (1, 2, 3), (1, 1, 1), (3, 1, 0),
    (2, 2, 1), (2, 2, 3), (2, 1, 0), (2, 3, 1), (1, 2, 1), (1, 1, 2),
    (2, 2, 0), (1, 3, 3), (2, 3, 3), (2, 2, 2), (1, 2, 0), (1, 3, 1),
    (2, 3, 0), (1, 4, 3), (1, 4, 1), (1, 2, 2), (1, 3, 0), (0, 0, 1),
    (2, 3, 2), (1, 4, 0), (1, 3, 2), (0, 0, 0), (0, 0, 3), (1, 4, 2),
    (0, 0, 2),
)


def swapped(value, axis, bit):
    return lax.ppermute(value, axis, [(i, i ^ 1 << bit) for i in range(lax.axis_size(axis))])


def dot(a, b):
    return jnp.dot(a, b, preferred_element_type=jnp.float32)


def small(mib=12):
    return pltpu.CompilerParams(vmem_limit_bytes=mib * 1024 * 1024)


def cost(products, shape):
    nodes, leaf, width = shape
    return pl.CostEstimate(
        flops=2 * products * nodes * leaf * leaf * width,
        bytes_accessed=2 * nodes * leaf * (2 * width + products * leaf),
        transcendentals=0,
    )


def first_source(field, one, two, level, chunk, width):
    nodes, leaf = one.shape[2:4]

    def kernel(x_ref, one_ref, two_ref, o_ref, x_held, one_held, two_held, sem):
        rows = field.shape[2] // nodes
        pieces = []
        for n in range(nodes):
            at = pl.ds(n * rows, rows)
            pieces.append((x_ref.at[0, 0, at], x_held.at[0, 0, at]))
        pieces.append((one_ref, one_held))
        pieces.append((two_ref, two_held))
        copies = [
            pltpu.make_async_copy(*piece, sem.at[i]) for i, piece in enumerate(pieces)
        ]
        for copy in copies:
            copy.start()
        for copy in copies:
            copy.wait()
        held = one_held if level == 1 else two_held
        for n in range(nodes):
            x = x_held[0, 0, pl.ds(n * leaf, leaf), pl.ds(chunk * width, width)]
            o_ref[n] = dot(held[0, 0, n], x).astype(o_ref.dtype)

    out = jax.ShapeDtypeStruct((nodes, leaf, width), jnp.bfloat16)
    like = [jax.ShapeDtypeStruct(a.shape, a.dtype) for a in (field, one, two)]
    return pl.pallas_call(
        kernel, out_shape=[out, *like], in_specs=[HBM] * 3, out_specs=[VMEM] * 4,
        scratch_shapes=[pltpu.SemaphoreType.DMA((nodes + 2,))],
        cost_estimate=cost(1, out.shape), compiler_params=small(),
    )(*[pltpu.with_memory_space_constraint(a, pltpu.HBM) for a in (field, one, two)])


def source(field, basis, chunk, width):
    nodes, leaf = basis.shape[2:4]

    def kernel(x_ref, s_ref, o_ref):
        for n in range(nodes):
            x = x_ref[0, 0, pl.ds(n * leaf, leaf), pl.ds(chunk * width, width)]
            o_ref[n] = dot(s_ref[0, 0, n], x).astype(o_ref.dtype)

    out = jax.ShapeDtypeStruct((nodes, leaf, width), jnp.bfloat16)
    return pl.pallas_call(
        kernel, out_shape=out, in_specs=[VMEM, VMEM], out_specs=VMEM,
        cost_estimate=cost(1, out.shape), compiler_params=small(),
    )(field, basis)


def advance(own, partner, weights, at, table, level, section):
    nodes, leaf, _ = own.shape

    def kernel(table_ref, own_ref, partner_ref, w_ref, o_ref):
        for n in range(nodes):
            w = w_ref[0, 0, at, n]
            other = partner_ref[table_ref[level, section, n]]
            total = dot(w[:, :leaf], own_ref[n]) + dot(w[:, leaf:], other)
            o_ref[n] = total.astype(o_ref.dtype)

    return pl.pallas_call(
        kernel, out_shape=jax.ShapeDtypeStruct(own.shape, own.dtype),
        in_specs=[SMEM, VMEM, VMEM, VMEM], out_specs=VMEM,
        cost_estimate=cost(2, own.shape), compiler_params=small(),
    )(table, own, partner, weights)


def target(sibling, distant, one, two, chunk, shape, held):
    nodes, leaf, width = sibling.shape

    def kernel(a_ref, b_ref, one_ref, two_ref, *refs):
        o_ref = refs[-1]
        for n in range(nodes):
            total = dot(one_ref[0, 0, n], a_ref[n]) + dot(two_ref[0, 0, n], b_ref[n])
            o_ref[0, 0, pl.ds(n * leaf, leaf), :] = total.astype(o_ref.dtype)

    args = (sibling, distant, one, two)
    specs = [VMEM] * 4
    alias = {}
    if held is not None:
        args += (held,)
        specs.append(pl.BlockSpec(memory_space=pl.ANY))
        alias = {4: 0}
    return pl.pallas_call(
        kernel, grid=(1,), out_shape=jax.ShapeDtypeStruct(shape, jnp.bfloat16),
        in_specs=specs,
        out_specs=pl.BlockSpec((1, 1, nodes * leaf, width), lambda i: (0, 0, 0, chunk)),
        input_output_aliases=alias,
        cost_estimate=cost(2, sibling.shape), compiler_params=small(),
    )(*args)


def on_device(
    field, source_one, sections_one, target_one, source_two, sections_two, target_two, pairing
):
    shape = field.shape
    width = shape[3] // CHUNKS
    top = lax.axis_size("grp").bit_length() - 1
    tables = pairing[:, :, 0, 0]
    sources = {1: source_one, 2: source_two}
    value, moved = {}, {}
    out = None
    for step in ORDER:
        level, stage, k = step
        axis, bit = "half", 0
        sent = None
        if level == 0:
            out = target(
                value[1, k], moved[2, k], target_one, target_two, k, shape, out
            )
        elif level == 3:
            sent = pairing if stage == 2 else sections_one[:, :, stage + 1 : stage + 2]
        elif stage == 0:
            if value:
                sent = source(field, sources[level], k, width)
            else:
                sent, field, sources[1], sources[2] = first_source(
                    field, source_one, source_two, level, k, width
                )
            value[level, k] = sent
            axis, bit = "grp", top - level
        elif level == 2:
            sent = value[2, k] = advance(
                value[2, k], moved[2, k], sections_two, stage - 1, tables, 1, stage - 1
            )
            axis, bit = "grp", top - 2 - stage if stage < 3 else top - 1
        elif stage == 1:
            sent = value[1, k] = advance(
                value[1, k], moved[1, k], sections_one, 0, tables, 0, 0
            )
        elif stage == 2:
            sent = value[1, k] = moved[1, k]
            axis, bit = "grp", top - 2
        else:
            value[1, k] = advance(
                value[1, k], moved[1, k], moved[3, stage - 3], 0,
                moved[3, 2][:, :, 0, 0], 0, stage - 2,
            )
            if stage == 3:
                sent = value[1, k]
                axis, bit = "grp", top - 3
        if sent is not None:
            result = swapped(sent, axis, bit)
            moved[(level, stage) if level == 3 else (level, k)] = result
    return out


def solution(mesh):
    placed = (
        P("grp", "half", None, None),
        P("grp", "half", None, None, None),
        P("grp", "half", None, None, None, None),
        P("grp", "half", None, None, None),
        P("grp", "half", None, None, None),
        P("grp", "half", None, None, None, None),
        P("grp", "half", None, None, None),
        P(None, None, "grp", "half", None),
    )
    return jax.shard_map(
        on_device,
        mesh=mesh,
        in_specs=placed,
        out_specs=P("grp", "half", None, None),
        check_vma=False,
    )
```

```python
import jax
import jax.numpy as jnp
from jax import lax
from jax.experimental import pallas as pl
from jax.experimental.pallas import tpu as pltpu
from jax.sharding import PartitionSpec as P


CHUNKS = 4
VMEM = pl.BlockSpec(memory_space=pltpu.VMEM)
HBM = pl.BlockSpec(memory_space=pltpu.HBM)
ORDER = (
    (2, 0, 0), (1, 0, 0), (2, 0, 2), (3, 0, 0), (1, 0, 2), (2, 0, 3),
    (3, 2, 0), (1, 0, 3), (2, 0, 1), (2, 1, 0), (2, 2, 0), (1, 1, 2),
    (1, 1, 0), (2, 1, 2), (1, 0, 1), (1, 2, 2), (2, 1, 3), (1, 1, 3),
    (2, 2, 2), (1, 2, 0), (2, 1, 1), (2, 3, 0), (2, 3, 2), (1, 1, 1),
    (3, 1, 0), (2, 2, 3), (1, 2, 3), (1, 3, 0), (1, 3, 2), (2, 3, 3),
    (1, 2, 1), (2, 2, 1), (1, 3, 3), (2, 3, 1), (1, 4, 2), (1, 3, 1),
    (1, 4, 3), (0, 0, 2), (1, 4, 0), (0, 0, 3), (0, 0, 0), (1, 4, 1),
    (0, 0, 1),
)


def swapped(value, axis, bit):
    return lax.ppermute(value, axis, [(i, i ^ 1 << bit) for i in range(lax.axis_size(axis))])


def dot(a, b):
    return jnp.dot(a, b, preferred_element_type=jnp.float32)


def small(mib=12):
    return pltpu.CompilerParams(vmem_limit_bytes=mib * 1024 * 1024)


def cost(products, shape):
    nodes, leaf, width = shape
    return pl.CostEstimate(
        flops=2 * products * nodes * leaf * leaf * width,
        bytes_accessed=2 * nodes * leaf * (2 * width + products * leaf),
        transcendentals=0,
    )


def first_source(field, one, two, level, chunk, width):
    nodes, leaf = one.shape[2:4]

    def kernel(x_ref, one_ref, two_ref, o_ref, x_held, one_held, two_held, sem):
        rows = field.shape[2] // nodes
        held = one_held if level == 1 else two_held
        needed = (one_ref if level == 1 else two_ref, held)
        later = (two_ref, two_held) if level == 1 else (one_ref, one_held)
        pieces = [needed]
        for n in range(nodes):
            at = pl.ds(n * rows, rows)
            pieces.append((x_ref.at[0, 0, at], x_held.at[0, 0, at]))
        pieces.append(later)
        copies = [
            pltpu.make_async_copy(*piece, sem.at[i]) for i, piece in enumerate(pieces)
        ]
        for copy in copies:
            copy.start()
        copies[0].wait()
        for n in range(nodes):
            copies[n + 1].wait()
            x = x_held[0, 0, pl.ds(n * leaf, leaf), pl.ds(chunk * width, width)]
            o_ref[n] = dot(held[0, 0, n], x).astype(o_ref.dtype)
        copies[-1].wait()

    out = jax.ShapeDtypeStruct((nodes, leaf, width), jnp.bfloat16)
    like = [jax.ShapeDtypeStruct(a.shape, a.dtype) for a in (field, one, two)]
    return pl.pallas_call(
        kernel, out_shape=[out, *like], in_specs=[HBM] * 3, out_specs=[VMEM] * 4,
        scratch_shapes=[pltpu.SemaphoreType.DMA((nodes + 2,))],
        cost_estimate=cost(1, out.shape), compiler_params=small(),
    )(*[pltpu.with_memory_space_constraint(a, pltpu.HBM) for a in (field, one, two)])


def source(field, basis, chunk, width):
    nodes, leaf = basis.shape[2:4]

    def kernel(x_ref, s_ref, o_ref):
        for n in range(nodes):
            x = x_ref[0, 0, pl.ds(n * leaf, leaf), pl.ds(chunk * width, width)]
            o_ref[n] = dot(s_ref[0, 0, n], x).astype(o_ref.dtype)

    out = jax.ShapeDtypeStruct((nodes, leaf, width), jnp.bfloat16)
    return pl.pallas_call(
        kernel, out_shape=out, in_specs=[VMEM, VMEM], out_specs=VMEM,
        cost_estimate=cost(1, out.shape), compiler_params=small(),
    )(field, basis)


def advance(own, partner, weights, at, table, level, section):
    nodes, leaf, _ = own.shape

    def kernel(table_ref, own_ref, partner_ref, w_ref, o_ref):
        for n in range(nodes):
            w = w_ref[0, 0, at, n]
            other = partner_ref[table_ref[level, section, 0, 0, n]]
            total = dot(w[:, :leaf], own_ref[n]) + dot(w[:, leaf:], other)
            o_ref[n] = total.astype(o_ref.dtype)

    return pl.pallas_call(
        kernel, out_shape=jax.ShapeDtypeStruct(own.shape, own.dtype),
        in_specs=[VMEM] * 4, out_specs=VMEM,
        cost_estimate=cost(2, own.shape), compiler_params=small(),
    )(table, own, partner, weights)


def target(sibling, distant, one, two, chunk, shape, held):
    nodes, leaf, width = sibling.shape

    def kernel(a_ref, b_ref, one_ref, two_ref, *refs):
        o_ref, z_ref, sem = refs[-3:]
        copies = []
        for n in range(nodes):
            total = dot(one_ref[0, 0, n], a_ref[n]) + dot(two_ref[0, 0, n], b_ref[n])
            z_ref[n] = total.astype(z_ref.dtype)
            piece = o_ref.at[0, 0, pl.ds(n * leaf, leaf), pl.ds(chunk * width, width)]
            copies.append(pltpu.make_async_copy(z_ref.at[n], piece, sem.at[n]))
            copies[n].start()
        for copy in copies:
            copy.wait()

    args = (sibling, distant, one, two)
    specs = [VMEM] * 4
    alias = {}
    if held is not None:
        args += (held,)
        specs.append(HBM)
        alias = {4: 0}
    return pl.pallas_call(
        kernel, out_shape=jax.ShapeDtypeStruct(shape, jnp.bfloat16),
        in_specs=specs, out_specs=HBM, input_output_aliases=alias,
        scratch_shapes=[
            pltpu.VMEM((nodes, leaf, width), jnp.bfloat16),
            pltpu.SemaphoreType.DMA((nodes,)),
        ],
        cost_estimate=cost(2, sibling.shape), compiler_params=small(),
    )(*args)


def on_device(
    field, source_one, sections_one, target_one, source_two, sections_two, target_two, pairing
):
    shape = field.shape
    width = shape[3] // CHUNKS
    top = lax.axis_size("grp").bit_length() - 1
    sources = {1: source_one, 2: source_two}
    value, moved = {}, {}
    out = None
    for step in ORDER:
        level, stage, k = step
        axis, bit = "half", 0
        sent = None
        if level == 0:
            out = target(
                value[1, k], moved[2, k], target_one, target_two, k, shape, out
            )
        elif level == 3:
            sent = pairing if stage == 2 else sections_one[:, :, stage + 1 : stage + 2]
        elif stage == 0:
            if value:
                sent = source(field, sources[level], k, width)
            else:
                sent, field, sources[1], sources[2] = first_source(
                    field, source_one, source_two, level, k, width
                )
            value[level, k] = sent
            axis, bit = "grp", top - level
        elif level == 2:
            sent = value[2, k] = advance(
                value[2, k], moved[2, k], sections_two, stage - 1, pairing, 1, stage - 1
            )
            axis, bit = "grp", top - 2 - stage if stage < 3 else top - 1
        elif stage == 1:
            sent = value[1, k] = advance(
                value[1, k], moved[1, k], sections_one, 0, pairing, 0, 0
            )
        elif stage == 2:
            sent = value[1, k] = moved[1, k]
            axis, bit = "grp", top - 2
        else:
            value[1, k] = advance(
                value[1, k], moved[1, k], moved[3, stage - 3], 0,
                moved[3, 2], 0, stage - 2,
            )
            if stage == 3:
                sent = value[1, k]
                axis, bit = "grp", top - 3
        if sent is not None:
            result = swapped(sent, axis, bit)
            moved[(level, stage) if level == 3 else (level, k)] = result
    return out


def solution(mesh):
    placed = (
        P("grp", "half", None, None),
        P("grp", "half", None, None, None),
        P("grp", "half", None, None, None, None),
        P("grp", "half", None, None, None),
        P("grp", "half", None, None, None),
        P("grp", "half", None, None, None, None),
        P("grp", "half", None, None, None),
        P(None, None, "grp", "half", None),
    )
    return jax.shard_map(
        on_device,
        mesh=mesh,
        in_specs=placed,
        out_specs=P("grp", "half", None, None),
        check_vma=False,
    )
```

```python
import jax
import jax.numpy as jnp
from jax import lax
from jax.experimental import pallas as pl
from jax.experimental.pallas import tpu as pltpu
from jax.sharding import PartitionSpec as P


CHUNKS = 4
VMEM = pl.BlockSpec(memory_space=pltpu.VMEM)
HBM = pl.BlockSpec(memory_space=pltpu.HBM)
ORDER = (
    (2, 0, 2), (1, 0, 0), (2, 0, 1), (1, 0, 1), (3, 0, 0), (2, 0, 3),
    (1, 1, 0), (2, 0, 0), (2, 1, 1), (1, 0, 2), (1, 0, 3), (2, 2, 1),
    (2, 1, 2), (1, 1, 1), (1, 2, 0), (3, 2, 0), (2, 2, 2), (1, 1, 2),
    (2, 1, 0), (2, 1, 3), (2, 3, 2), (1, 2, 1), (1, 1, 3), (3, 1, 0),
    (2, 3, 1), (1, 3, 0), (2, 2, 0), (1, 2, 2), (1, 3, 1), (2, 3, 0),
    (1, 2, 3), (2, 2, 3), (1, 3, 2), (2, 3, 3), (1, 4, 0), (1, 3, 3),
    (1, 4, 1), (0, 0, 0), (0, 0, 1), (1, 4, 2), (0, 0, 2), (1, 4, 3),
    (0, 0, 3),
)


def swapped(value, axis, bit):
    return lax.ppermute(value, axis, [(i, i ^ 1 << bit) for i in range(lax.axis_size(axis))])


def dot(a, b):
    return jnp.dot(a, b, preferred_element_type=jnp.float32)


def small(mib=12):
    return pltpu.CompilerParams(vmem_limit_bytes=mib * 1024 * 1024)


def cost(products, shape):
    nodes, leaf, width = shape
    return pl.CostEstimate(
        flops=2 * products * nodes * leaf * leaf * width,
        bytes_accessed=2 * nodes * leaf * (2 * width + products * leaf),
        transcendentals=0,
    )


def first_source(field, one, two, level, chunk, width):
    nodes, leaf = one.shape[2:4]

    def kernel(x_ref, one_ref, two_ref, o_ref, x_held, one_held, two_held, sem):
        rows = field.shape[2] // nodes
        held = one_held if level == 1 else two_held
        needed = (one_ref if level == 1 else two_ref, held)
        later = (two_ref, two_held) if level == 1 else (one_ref, one_held)
        pieces = [needed]
        for n in range(nodes):
            at = pl.ds(n * rows, rows)
            pieces.append((x_ref.at[0, 0, at], x_held.at[0, 0, at]))
        pieces.append(later)
        copies = [
            pltpu.make_async_copy(*piece, sem.at[i]) for i, piece in enumerate(pieces)
        ]
        for copy in copies:
            copy.start()
        copies[0].wait()
        for n in range(nodes):
            copies[n + 1].wait()
            x = x_held[0, 0, pl.ds(n * leaf, leaf), pl.ds(chunk * width, width)]
            o_ref[n] = dot(held[0, 0, n], x).astype(o_ref.dtype)
        copies[-1].wait()

    out = jax.ShapeDtypeStruct((nodes, leaf, width), jnp.bfloat16)
    like = [jax.ShapeDtypeStruct(a.shape, a.dtype) for a in (field, one, two)]
    return pl.pallas_call(
        kernel, out_shape=[out, *like], in_specs=[HBM] * 3, out_specs=[VMEM] * 4,
        scratch_shapes=[pltpu.SemaphoreType.DMA((nodes + 2,))],
        cost_estimate=cost(1, out.shape), compiler_params=small(),
    )(*[pltpu.with_memory_space_constraint(a, pltpu.HBM) for a in (field, one, two)])


def source(field, basis, chunk, width):
    nodes, leaf = basis.shape[2:4]

    def kernel(x_ref, s_ref, o_ref):
        for n in range(nodes):
            x = x_ref[0, 0, pl.ds(n * leaf, leaf), pl.ds(chunk * width, width)]
            o_ref[n] = dot(s_ref[0, 0, n], x).astype(o_ref.dtype)

    out = jax.ShapeDtypeStruct((nodes, leaf, width), jnp.bfloat16)
    return pl.pallas_call(
        kernel, out_shape=out, in_specs=[VMEM, VMEM], out_specs=VMEM,
        cost_estimate=cost(1, out.shape), compiler_params=small(),
    )(field, basis)


def advance(own, partner, weights, at, table, level, section):
    nodes, leaf, _ = own.shape

    def kernel(table_ref, own_ref, partner_ref, w_ref, o_ref):
        for n in range(nodes):
            w = w_ref[0, 0, at, n]
            other = partner_ref[table_ref[level, section, 0, 0, n]]
            total = dot(w[:, :leaf], own_ref[n]) + dot(w[:, leaf:], other)
            o_ref[n] = total.astype(o_ref.dtype)

    return pl.pallas_call(
        kernel, out_shape=jax.ShapeDtypeStruct(own.shape, own.dtype),
        in_specs=[VMEM] * 4, out_specs=VMEM,
        cost_estimate=cost(2, own.shape), compiler_params=small(),
    )(table, own, partner, weights)


def target(sibling, distant, one, two, chunk, shape, ready):
    nodes, leaf, width = sibling.shape

    def product(a_ref, b_ref, one_ref, two_ref, z_ref, n):
        total = dot(one_ref[0, 0, n], a_ref[n]) + dot(two_ref[0, 0, n], b_ref[n])
        z_ref[n] = total.astype(z_ref.dtype)

    def early(*refs):
        for n in range(nodes):
            product(*refs, n)

    def last(*refs):
        o_ref, z_ref, sem, ready_sem = refs[-4:]
        copies = []
        for i, (k, _) in enumerate(ready):
            for n in range(nodes):
                piece = o_ref.at[0, 0, pl.ds(n * leaf, leaf), pl.ds(k * width, width)]
                copy = pltpu.make_async_copy(refs[4 + i].at[n], piece, ready_sem.at[i, n])
                copies.append(copy)
                copy.start()
        for n in range(nodes):
            product(*refs[:4], z_ref, n)
            piece = o_ref.at[0, 0, pl.ds(n * leaf, leaf), pl.ds(chunk * width, width)]
            copy = pltpu.make_async_copy(z_ref.at[n], piece, sem.at[n])
            copies.append(copy)
            copy.start()
        for copy in copies:
            copy.wait()

    args = (sibling, distant, one, two)
    if len(ready) < CHUNKS - 1:
        return pl.pallas_call(
            early, out_shape=jax.ShapeDtypeStruct(sibling.shape, jnp.bfloat16),
            in_specs=[VMEM] * 4, out_specs=VMEM,
            cost_estimate=cost(2, sibling.shape), compiler_params=small(),
        )(*args)
    args += tuple(value for _, value in ready)
    return pl.pallas_call(
        last, out_shape=jax.ShapeDtypeStruct(shape, jnp.bfloat16),
        in_specs=[VMEM] * len(args), out_specs=HBM,
        scratch_shapes=[
            pltpu.VMEM((nodes, leaf, width), jnp.bfloat16),
            pltpu.SemaphoreType.DMA((nodes,)),
            pltpu.SemaphoreType.DMA((len(ready), nodes)),
        ],
        cost_estimate=cost(2, sibling.shape), compiler_params=small(),
    )(*args)


def on_device(
    field, source_one, sections_one, target_one, source_two, sections_two, target_two, pairing
):
    shape = field.shape
    width = shape[3] // CHUNKS
    top = lax.axis_size("grp").bit_length() - 1
    sources = {1: source_one, 2: source_two}
    value, moved = {}, {}
    out, ready = None, []
    for step in ORDER:
        level, stage, k = step
        axis, bit = "half", 0
        sent = None
        if level == 0:
            out = target(
                value[1, k], moved[2, k], target_one, target_two, k, shape, ready
            )
            ready.append((k, out))
        elif level == 3:
            sent = pairing if stage == 2 else sections_one[:, :, stage + 1 : stage + 2]
        elif stage == 0:
            if value:
                sent = source(field, sources[level], k, width)
            else:
                sent, field, sources[1], sources[2] = first_source(
                    field, source_one, source_two, level, k, width
                )
            value[level, k] = sent
            axis, bit = "grp", top - level
        elif level == 2:
            sent = value[2, k] = advance(
                value[2, k], moved[2, k], sections_two, stage - 1, pairing, 1, stage - 1
            )
            axis, bit = "grp", top - 2 - stage if stage < 3 else top - 1
        elif stage == 1:
            sent = value[1, k] = advance(value[1, k], moved[1, k], sections_one, 0, pairing, 0, 0)
        elif stage == 2:
            sent = value[1, k] = moved[1, k]
            axis, bit = "grp", top - 2
        else:
            value[1, k] = advance(
                value[1, k], moved[1, k], moved[3, stage - 3], 0,
                moved[3, 2], 0, stage - 2,
            )
            if stage == 3:
                sent = value[1, k]
                axis, bit = "grp", top - 3
        if sent is not None:
            result = swapped(sent, axis, bit)
            moved[(level, stage) if level == 3 else (level, k)] = result
    return out


def solution(mesh):
    placed = (
        P("grp", "half", None, None),
        P("grp", "half", None, None, None),
        P("grp", "half", None, None, None, None),
        P("grp", "half", None, None, None),
        P("grp", "half", None, None, None),
        P("grp", "half", None, None, None, None),
        P("grp", "half", None, None, None),
        P(None, None, "grp", "half", None),
    )
    return jax.shard_map(
        on_device,
        mesh=mesh,
        in_specs=placed,
        out_specs=P("grp", "half", None, None),
        check_vma=False,
    )
```

```python
import jax
import jax.numpy as jnp
from jax import lax
from jax.experimental import pallas as pl
from jax.experimental.pallas import tpu as pltpu
from jax.sharding import PartitionSpec as P


CHUNKS = 4
VMEM = pl.BlockSpec(memory_space=pltpu.VMEM)
HBM = pl.BlockSpec(memory_space=pltpu.HBM)
ORDER = (
    (2, 0, 2), (1, 0, 0), (2, 0, 1), (1, 0, 1), (3, 0, 0), (2, 0, 3),
    (1, 1, 0), (2, 0, 0), (2, 1, 1), (1, 0, 2), (1, 0, 3), (2, 2, 1),
    (2, 1, 2), (1, 1, 1), (1, 2, 0), (3, 2, 0), (2, 2, 2), (1, 1, 2),
    (2, 1, 0), (2, 1, 3), (2, 3, 2), (1, 2, 1), (1, 1, 3), (3, 1, 0),
    (2, 3, 1), (2, 2, 0), (1, 2, 2), (1, 3, 1), (1, 3, 0), (2, 3, 0),
    (1, 2, 3), (2, 2, 3), (1, 3, 2), (2, 3, 3), (1, 4, 0), (1, 3, 3),
    (1, 4, 1), (0, 0, 0), (0, 0, 1), (1, 4, 2), (0, 0, 2), (1, 4, 3),
    (0, 0, 3),
)


def swapped(value, axis, bit):
    return lax.ppermute(value, axis, [(i, i ^ 1 << bit) for i in range(lax.axis_size(axis))])


def dot(a, b):
    return jnp.dot(a, b, preferred_element_type=jnp.float32)


def small(mib=12):
    return pltpu.CompilerParams(vmem_limit_bytes=mib * 1024 * 1024)


def cost(products, shape):
    nodes, leaf, width = shape
    return pl.CostEstimate(
        flops=2 * products * nodes * leaf * leaf * width,
        bytes_accessed=2 * nodes * leaf * (2 * width + products * leaf),
        transcendentals=0,
    )


def first_source(field, one, two, level, chunk, width):
    nodes, leaf = one.shape[2:4]

    def kernel(x_ref, one_ref, two_ref, o_ref, x_held, one_held, two_held, sem):
        rows = field.shape[2] // nodes
        held = one_held if level == 1 else two_held
        needed = (one_ref if level == 1 else two_ref, held)
        later = (two_ref, two_held) if level == 1 else (one_ref, one_held)
        pieces = [needed]
        for n in range(nodes):
            at = pl.ds(n * rows, rows)
            pieces.append((x_ref.at[0, 0, at], x_held.at[0, 0, at]))
        pieces.append(later)
        copies = [
            pltpu.make_async_copy(*piece, sem.at[i]) for i, piece in enumerate(pieces)
        ]
        for copy in copies:
            copy.start()
        copies[0].wait()
        for n in range(nodes):
            copies[n + 1].wait()
            x = x_held[0, 0, pl.ds(n * leaf, leaf), pl.ds(chunk * width, width)]
            o_ref[n] = dot(held[0, 0, n], x).astype(o_ref.dtype)
        copies[-1].wait()

    out = jax.ShapeDtypeStruct((nodes, leaf, width), jnp.bfloat16)
    like = [jax.ShapeDtypeStruct(a.shape, a.dtype) for a in (field, one, two)]
    return pl.pallas_call(
        kernel, out_shape=[out, *like], in_specs=[HBM] * 3, out_specs=[VMEM] * 4,
        scratch_shapes=[pltpu.SemaphoreType.DMA((nodes + 2,))],
        cost_estimate=cost(1, out.shape), compiler_params=small(),
    )(*[pltpu.with_memory_space_constraint(a, pltpu.HBM) for a in (field, one, two)])


def source(field, basis, chunk, width):
    nodes, leaf = basis.shape[2:4]

    def kernel(x_ref, s_ref, o_ref):
        for n in range(nodes):
            x = x_ref[0, 0, pl.ds(n * leaf, leaf), pl.ds(chunk * width, width)]
            o_ref[n] = dot(s_ref[0, 0, n], x).astype(o_ref.dtype)

    out = jax.ShapeDtypeStruct((nodes, leaf, width), jnp.bfloat16)
    return pl.pallas_call(
        kernel, out_shape=out, in_specs=[VMEM, VMEM], out_specs=VMEM,
        cost_estimate=cost(1, out.shape), compiler_params=small(),
    )(field, basis)


def advance(own, partner, weights, at, table, level, section):
    nodes, leaf, _ = own.shape

    def kernel(table_ref, own_ref, partner_ref, w_ref, o_ref):
        for n in range(nodes):
            w = w_ref[0, 0, at, n]
            other = partner_ref[table_ref[level, section, 0, 0, n]]
            total = dot(w[:, :leaf], own_ref[n]) + dot(w[:, leaf:], other)
            o_ref[n] = total.astype(o_ref.dtype)

    return pl.pallas_call(
        kernel, out_shape=jax.ShapeDtypeStruct(own.shape, own.dtype),
        in_specs=[VMEM] * 4, out_specs=VMEM,
        cost_estimate=cost(2, own.shape), compiler_params=small(),
    )(table, own, partner, weights)


def target(sibling, distant, one, two, chunk, shape, ready):
    nodes, leaf, width = sibling.shape

    def product(a_ref, b_ref, one_ref, two_ref, z_ref, n):
        total = dot(one_ref[0, 0, n], a_ref[n]) + dot(two_ref[0, 0, n], b_ref[n])
        z_ref[n] = total.astype(z_ref.dtype)

    def early(*refs):
        for n in range(nodes):
            product(*refs, n)

    def last(*refs):
        o_ref, z_ref, sem, ready_sem = refs[-4:]
        copies = []
        for i, (k, _) in enumerate(ready):
            for n in range(nodes):
                piece = o_ref.at[0, 0, pl.ds(n * leaf, leaf), pl.ds(k * width, width)]
                copy = pltpu.make_async_copy(refs[4 + i].at[n], piece, ready_sem.at[i, n])
                copies.append(copy)
                copy.start()
        for n in range(nodes):
            product(*refs[:4], z_ref, n)
            piece = o_ref.at[0, 0, pl.ds(n * leaf, leaf), pl.ds(chunk * width, width)]
            copy = pltpu.make_async_copy(z_ref.at[n], piece, sem.at[n])
            copies.append(copy)
            copy.start()
        for copy in copies:
            copy.wait()

    args = (sibling, distant, one, two)
    final = len(ready) == CHUNKS - 1
    if len(ready) < CHUNKS - 2:
        return pl.pallas_call(
            early, out_shape=jax.ShapeDtypeStruct(sibling.shape, jnp.bfloat16),
            in_specs=[VMEM] * 4, out_specs=VMEM,
            cost_estimate=cost(2, sibling.shape), compiler_params=small(),
        )(*args)
    alias = {}
    specs = [VMEM] * (4 + len(ready))
    if final:
        args += (ready[-1][1],)
        specs, alias, ready = [VMEM] * 4 + [HBM], {4: 0}, []
    else:
        args += tuple(value for _, value in ready)
    return pl.pallas_call(
        last, out_shape=jax.ShapeDtypeStruct(shape, jnp.bfloat16),
        in_specs=specs, out_specs=HBM, input_output_aliases=alias,
        scratch_shapes=[
            pltpu.VMEM((nodes, leaf, width), jnp.bfloat16),
            pltpu.SemaphoreType.DMA((nodes,)),
            pltpu.SemaphoreType.DMA((max(len(ready), 1), nodes)),
        ],
        cost_estimate=cost(2, sibling.shape), compiler_params=small(),
    )(*args)


def on_device(
    field, source_one, sections_one, target_one, source_two, sections_two, target_two, pairing
):
    shape = field.shape
    width = shape[3] // CHUNKS
    top = lax.axis_size("grp").bit_length() - 1
    sources = {1: source_one, 2: source_two}
    value, moved = {}, {}
    out, ready = None, []
    for step in ORDER:
        level, stage, k = step
        axis, bit = "half", 0
        sent = None
        if level == 0:
            out = target(
                value[1, k], moved[2, k], target_one, target_two, k, shape, ready
            )
            ready.append((k, out))
        elif level == 3:
            sent = pairing if stage == 2 else sections_one[:, :, stage + 1 : stage + 2]
        elif stage == 0:
            if value:
                sent = source(field, sources[level], k, width)
            else:
                sent, field, sources[1], sources[2] = first_source(
                    field, source_one, source_two, level, k, width
                )
            value[level, k] = sent
            axis, bit = "grp", top - level
        elif level == 2:
            sent = value[2, k] = advance(
                value[2, k], moved[2, k], sections_two, stage - 1, pairing, 1, stage - 1
            )
            axis, bit = "grp", top - 2 - stage if stage < 3 else top - 1
        elif stage == 1:
            sent = value[1, k] = advance(
                value[1, k], moved[1, k], sections_one, 0, pairing, 0, 0
            )
        elif stage == 2:
            sent = value[1, k] = moved[1, k]
            axis, bit = "grp", top - 2
        else:
            value[1, k] = advance(
                value[1, k], moved[1, k], moved[3, stage - 3], 0,
                moved[3, 2], 0, stage - 2,
            )
            if stage == 3:
                sent = value[1, k]
                axis, bit = "grp", top - 3
        if sent is not None:
            result = swapped(sent, axis, bit)
            moved[(level, stage) if level == 3 else (level, k)] = result
    return out


def solution(mesh):
    placed = (
        P("grp", "half", None, None),
        P("grp", "half", None, None, None),
        P("grp", "half", None, None, None, None),
        P("grp", "half", None, None, None),
        P("grp", "half", None, None, None),
        P("grp", "half", None, None, None, None),
        P("grp", "half", None, None, None),
        P(None, None, "grp", "half", None),
    )
    return jax.shard_map(
        on_device,
        mesh=mesh,
        in_specs=placed,
        out_specs=P("grp", "half", None, None),
        check_vma=False,
    )
```
